256 devices in a mesh: orb: 8 (over y, core), aux: 32 (over x, z).
Axes of the slice: x: 4, y: 4, z: 8, core: 2. Of those that a mesh axis runs over, the one named last changes fastest.
Arguments:
- factors: bfloat16 [384, 128, 2048], P('orb', None, 'aux'), may hold values from -6 to 6
- amplitudes: bfloat16 [384, 12, 128, 128], P('orb'), may hold values from -0.15625 to 0.15625
- partners: int32 [384, 12], P('orb'), may hold values from 0 to 383, as said below
- metric_tiles: bfloat16 [128, 128, 128], P('aux'), may hold values from -0.1875 to 0.1875
- tile_pos: int32 [128, 2], P('aux'), may hold values from 0 to 15, as said below
Outputs:
- density: bfloat16 [384, 128, 2048], P('orb', 'aux')
The draws below stay inside these ranges and needn't reach their ends.
Inputs may be any that keep to these rules, and one draw needn't show every extreme that they name: partners[i, 0] = i for every orbital i; the other partners of an orbital are any orbitals, repeats allowed. `tile_pos`: the listed positions (row block, column block) are all distinct, and each of the 16 diagonal positions is listed.
All inputs are finite; a program needn't handle non-finite values.
Results may differ from the reference program's by a relative error of at most 0.0049.
Values may be sent and summed in bfloat16 or wider, within the bound.
A program may use at most 128 MiB of HBM per device.

```python
import jax
import jax.numpy as jnp
from jax import lax

NVD = 128
AUX = 2048
TILE = 128
PAIRS = 12
NTILE = 128
OCC = 384
NBLK = 16


def draw_partners(key, part):
    orbitals = jnp.arange(OCC, dtype=jnp.int32)
    others = jax.random.randint(jax.random.fold_in(key, 11), (OCC, PAIRS - 1), 0, OCC, dtype=jnp.int32)
    return jnp.concatenate([orbitals[:, None], others], axis=1).astype(jnp.int32)


def draw_tile_pos(key, part):
    cells = jnp.arange(NBLK * NBLK, dtype=jnp.int32)
    row_ids = cells // NBLK
    col_ids = cells % NBLK
    scores = jax.random.permutation(jax.random.fold_in(key, 21), NBLK * NBLK).astype(jnp.int32)
    scores = jnp.where(row_ids != col_ids, scores + 1, jnp.zeros_like(scores))
    order = jnp.argsort(scores, stable=True)[:NTILE]
    chosen = jnp.take(cells, order)
    shuffle = jax.random.permutation(jax.random.fold_in(key, 22), NTILE)
    chosen = jnp.take(chosen, shuffle)
    return jnp.stack([chosen // NBLK, chosen % NBLK], axis=1).astype(jnp.int32)


def block_levels(rng, shape, shards, low, high):
    gain, own = 1.0, jax.random.fold_in(rng, 6)
    for axis_at, shards_of in shards:
        draws = jnp.exp(jax.random.uniform(jax.random.fold_in(own, axis_at), (shards_of,), jnp.float32, low / len(shards), high / len(shards)))
        gain = gain * jnp.repeat(draws, shape[axis_at] // shards_of).reshape([-1 if axis == axis_at else 1 for axis in range(len(shape))])
    return gain


def normal_values(stream_key, extent, width, reach, split=(), kind=jnp.bfloat16):
    array = width * jax.random.normal(stream_key, extent, jnp.float32)
    if split:
        array = array * block_levels(stream_key, extent, split, -0.22, 0.18)
    return jnp.clip(array, -reach, reach).astype(kind)


def setup_inputs(seed: int = 0) -> dict:
    seeds = jax.random.split(jax.random.key(seed), 6)
    factors = normal_values(seeds[0], (OCC, NVD, AUX), 1.0, 6.0, ((0, 8), (2, 32)))
    amplitudes = normal_values(seeds[1], (OCC, PAIRS, NVD, NVD), (PAIRS * NVD) ** -0.5, 0.15625, ((0, 8),))
    partners = draw_partners(jax.random.fold_in(seeds[5], 71), 0)
    metric_tiles = normal_values(seeds[3], (NTILE, TILE, TILE), (TILE * NTILE // NBLK) ** -0.5, 0.1875, ((0, 32),))
    tile_pos = draw_tile_pos(jax.random.fold_in(seeds[5], 71), 0)
    return dict(factors=factors, amplitudes=amplitudes, partners=partners, metric_tiles=metric_tiles, tile_pos=tile_pos)


def reference(factors, amplitudes, partners, metric_tiles, tile_pos):
    def one_orbital(inputs):
        amp_tiles, partner_ids = inputs
        picked = jnp.take(factors, partner_ids, axis=0).astype(jnp.float32)
        summed = jnp.einsum("kab,kbp->ap", amp_tiles.astype(jnp.float32), picked, precision=lax.Precision.HIGHEST)
        return summed.astype(jnp.bfloat16)

    gammas = lax.map(one_orbital, (amplitudes, partners))
    full_metric = jnp.zeros((NBLK, NBLK, TILE, TILE), jnp.float32)
    full_metric = full_metric.at[tile_pos[:, 0], tile_pos[:, 1]].add(metric_tiles.astype(jnp.float32))
    full_metric = full_metric.transpose(0, 2, 1, 3).reshape(AUX, AUX)
    row_block = gammas.reshape(OCC * NVD, AUX).astype(jnp.float32)
    product = jnp.dot(row_block, full_metric, precision=lax.Precision.HIGHEST)
    return product.reshape(OCC, NVD, AUX).astype(jnp.bfloat16)
```

```python
import functools

import jax
import jax.numpy as jnp
from jax import lax
from jax.experimental import pallas as pl
from jax.experimental.pallas import tpu as pltpu
from jax.sharding import PartitionSpec as P

MESH = pl.DeviceIdType.MESH
NY, NX, NZ = 4, 4, 8
NAUX = NX * NZ
CHUNKS = 2
PIECES = 4
SUBS = 3
NBLK = 16
XPLUS = (0, 1, 2, 4)
XMINUS = (5, 6, 7, 3)


def kernel(ft, amp, part, tiles, meta, out, *scratch):
    fbuf = scratch[:CHUNKS]
    (ampv, mbuf, stage, sbuf, rbuf, lhs, inv_v, inv_s) = scratch[CHUNKS:CHUNKS + 8]
    (loc, ysend, ssend, yp, ym, y2p, y2m, sib,
     msend, rzp, rzm, rxp, rxm, rx2, msib, asend, arecv) = scratch[CHUNKS + 8:]

    o = lax.axis_index("orb")
    s = lax.axis_index("aux")
    y, h = o // 2, o % 2
    x, z = s // NZ, s % NZ
    own, npair = amp.shape[0], amp.shape[1]
    nt = tiles.shape[0]
    span = tiles.shape[1]
    half = nt // 2
    pw = ft.shape[1] // CHUNKS
    lanes = 128
    per = lanes // pw
    ng = own // per
    gl = ng // SUBS
    npc = own // PIECES
    nrow = ng * 4

    def orb_at(dy):
        return lax.rem(y + dy + NY, NY) * 2 + h

    def aux_at(dx, dz):
        return lax.rem(x + dx + NX, NX) * NZ + lax.rem(z + dz + NZ, NZ)

    sibling = (y * 2 + 1 - h, s)
    yplus, yminus = (orb_at(1), s), (orb_at(-1), s)
    xplus, xminus = (o, aux_at(1, 0)), (o, aux_at(-1, 0))
    zplus, zminus = (o, aux_at(0, 1)), (o, aux_at(0, -1))

    def remote(src, dst, ssem, rsem, dev):
        return pltpu.make_async_remote_copy(
            src_ref=src, dst_ref=dst, send_sem=ssem, recv_sem=rsem, device_id=dev, device_id_type=MESH)

    def recv(ref, ssem, rsem):
        remote(ref, ref, ssem, rsem, sibling).wait_recv()

    def sent(ref, ssem, rsem):
        remote(ref, ref, ssem, rsem, sibling).wait_send()

    mine = pl.ds(s * nt, nt)
    load_tiles = pltpu.make_async_copy(tiles, mbuf.at[mine, pl.ds(0, span)], loc.at[0])
    load_meta = pltpu.make_async_copy(meta, mbuf.at[mine, pl.ds(span, 16)], loc.at[1])
    load_tiles.start()
    load_meta.start()
    load_own = [
        pltpu.make_async_copy(ft.at[:, pl.ds(c * pw, pw), :], fbuf[c].at[pl.ds(o * own, own)], loc.at[2 + c])
        for c in range(CHUNKS)
    ]
    for copy in load_own:
        copy.start()
    load_amp = pltpu.make_async_copy(amp, ampv, loc.at[2 + CHUNKS])
    load_amp.start()

    barrier = pltpu.get_barrier_semaphore()
    for dev in (sibling, yplus, yminus, xplus, xminus, zplus, zminus):
        pl.semaphore_signal(barrier, inc=1, device_id=dev, device_id_type=MESH)
    pl.semaphore_wait(barrier, 7)

    def fpiece(c, orb, q):
        return fbuf[c].at[pl.ds(orb * own + q * npc, npc)]

    def to_sibling(c, ref):
        remote(ref, ref, ssend.at[c], sib.at[c], sibling).start()

    def gather_start(c):
        for q in range(PIECES):
            src = ft.at[pl.ds(q * npc, npc), pl.ds(c * pw, pw), :]
            dst = fpiece(c, o, q)
            remote(src, dst, ysend.at[c], yp.at[c, q], yplus).start()
            remote(src, dst, ysend.at[c], ym.at[c, q], yminus).start()
        for q in range(PIECES):
            src = ft.at[pl.ds(q * npc, npc), pl.ds(c * pw, pw), :]
            remote(src, fpiece(c, o, q), ssend.at[c], sib.at[c], sibling).start()

    def gather_round(c, q):
        below, above = fpiece(c, orb_at(-1), q), fpiece(c, orb_at(1), q)
        recv(below, ysend.at[c], yp.at[c, q])
        if q < PIECES // 2:
            remote(below, below, ysend.at[c], y2p.at[c, q], yplus).start()
        to_sibling(c, below)
        recv(above, ysend.at[c], ym.at[c, q])
        if q >= PIECES // 2:
            remote(above, above, ysend.at[c], y2m.at[c, q - PIECES // 2], yminus).start()
        to_sibling(c, above)

    def gather_far(c, q):
        far = fpiece(c, orb_at(2), q)
        if q < PIECES // 2:
            recv(far, ysend.at[c], y2p.at[c, q])
        else:
            recv(far, ysend.at[c], y2m.at[c, q - PIECES // 2])
        to_sibling(c, far)

    def gather_done(c):
        recv(fbuf[c].at[pl.ds(0, NY * own)], ssend.at[c], sib.at[c])
        load_own[c].wait()

    def shard(dx, idx):
        dz = -idx if idx <= NZ // 2 else idx - NZ // 2
        return mbuf.at[pl.ds(aux_at(dx, dz) * nt + h * half, half)]

    def tiles_out(idx):
        ref = shard(0, idx)
        if idx < NZ // 2:
            remote(ref, ref, msend.at[0], rzp.at[idx], zplus).start()
        if idx == 0:
            remote(ref, ref, msend.at[0], rzm.at[0], zminus).start()
        elif idx > NZ // 2 and idx < NZ - 1:
            remote(ref, ref, msend.at[0], rzm.at[idx - NZ // 2], zminus).start()
        remote(ref, ref, msend.at[1], rxp.at[idx], xplus).start()
        remote(ref, ref, msend.at[2], rxm.at[idx], xminus).start()
        if idx:
            remote(ref, ref, msend.at[3], msib.at[0], sibling).start()

    def tiles_x(idx):
        left, right = shard(-1, idx), shard(1, idx)
        recv(left, msend.at[1], rxp.at[idx])
        if idx in XPLUS:
            remote(left, left, msend.at[4], rx2.at[idx], xplus).start()
        remote(left, left, msend.at[3], msib.at[0], sibling).start()
        recv(right, msend.at[2], rxm.at[idx])
        if idx in XMINUS:
            remote(right, right, msend.at[4], rx2.at[idx], xminus).start()
        remote(right, right, msend.at[3], msib.at[0], sibling).start()

    def tiles_round(k):
        if k <= NZ // 2:
            recv(shard(0, k), msend.at[0], rzp.at[k - 1])
            tiles_out(k)
        if k < NZ // 2:
            recv(shard(0, NZ // 2 + k), msend.at[0], rzm.at[k - 1])
            tiles_out(NZ // 2 + k)
        tiles_x(k - 1)
        if k >= 2 and k - 1 < NZ // 2:
            tiles_x(NZ // 2 + k - 1)

    def tiles_far():
        for idx in range(NZ):
            far = shard(2, idx)
            recv(far, msend.at[4], rx2.at[idx])
            remote(far, far, msend.at[3], msib.at[0], sibling).start()
        recv(mbuf.at[pl.ds(0, (NAUX - 1) * half)], msend.at[3], msib.at[0])

    def contract(c, g):
        blank = {n: jnp.zeros((n * pw, lanes), jnp.bfloat16) for n in range(1, per)}
        left, right = [], []
        for k in range(npair):
            for q in range(per):
                i = q * ng + g
                left.append(ampv[i, k])
                rows = [fbuf[c][part[k, i]]]
                if q:
                    rows.insert(0, blank[q])
                if q < per - 1:
                    rows.append(blank[per - 1 - q])
                right.append(jnp.concatenate(rows, axis=0))
        return lax.dot_general(
            jnp.concatenate(left, axis=1), jnp.concatenate(right, axis=1),
            (((1,), (1,)), ((), ())), preferred_element_type=jnp.float32)

    def contract_sub(c, u):
        def body(g, carry):
            value = contract(c, u * gl + g)
            at = pl.multiple_of(g * 4, 4)
            for r in range(NAUX):
                stage[r, pl.ds(at, 4), :] = value[4 * r:4 * r + 4, :]
            return carry
        lax.fori_loop(0, gl, body, 0)
        rows = pl.ds(u * gl * 4, gl * 4)

        def pack(r, carry):
            sbuf[c, r, rows, :] = stage[r].astype(jnp.bfloat16)
            return carry
        lax.fori_loop(0, NAUX, pack, 0)

        def send(d, carry):
            to = lax.rem(s + d, NAUX)
            remote(sbuf.at[c, to, rows], rbuf.at[c, s, rows], asend.at[c, u], arecv.at[c, u], (o, to)).start()
            return carry
        lax.fori_loop(1, NAUX, send, 0)
        rbuf[c, s, rows, :] = sbuf[c, s, rows, :]

    load_tiles.wait()
    load_meta.wait()
    mbuf[NAUX * nt] = jnp.zeros(mbuf.shape[1:], jnp.bfloat16)
    gather_start(0)
    tiles_out(0)
    for q in range(PIECES):
        gather_round(0, q)
        tiles_round(q + 1)
    for c in range(1, CHUNKS):
        gather_start(c)
    for q in range(PIECES):
        gather_far(0, q)
    tiles_x(NZ // 2)
    tiles_far()
    gather_done(0)
    load_amp.wait()
    for c in range(CHUNKS):
        for u in range(SUBS):
            contract_sub(c, u)
            if c + 1 < CHUNKS:
                for q in range(PIECES):
                    if q * SUBS // PIECES == u:
                        gather_round(c + 1, q)
        if c + 1 < CHUNKS:
            for q in range(PIECES):
                gather_far(c + 1, q)
            gather_done(c + 1)

    def look(t, carry):
        low, high = carry
        key = mbuf[t, pl.ds(span, 16), :].astype(jnp.int32)
        lane = lax.broadcasted_iota(jnp.int32, key.shape, 1)
        return jnp.where(key == lane, t, low), jnp.where(key == lane + lanes, t, high)

    none = jnp.full((16, lanes), NAUX * nt, jnp.int32)
    low, high = lax.fori_loop(0, NAUX * nt, look, (none, none))
    inv_v[0] = low[0:8]
    inv_v[1] = high[0:8]
    copy = pltpu.make_async_copy(inv_v, inv_s, loc.at[3 + CHUNKS])
    copy.start()
    copy.wait()

    for c in range(CHUNKS):
        for u in range(SUBS):
            ref = rbuf.at[c, pl.ds(0, NAUX - 1), pl.ds(u * gl * 4, gl * 4)]
            recv(ref, asend.at[c, u], arecv.at[c, u])

    def arrange(b, carry):
        blocks = [rbuf[c, 2 * b + e] for e in range(2) for c in range(CHUNKS)]
        at = pl.multiple_of(b * lanes, lanes)
        for q in range(per):
            lhs[pl.ds(q * nrow, nrow), pl.ds(at, lanes)] = jnp.concatenate(
                [blk[:, q * pw:(q + 1) * pw] for blk in blocks], axis=1)
        return carry
    lax.fori_loop(0, NBLK, arrange, 0)

    def columns(cb, carry):
        rows = []
        for r in range(NBLK):
            pair = []
            for e in range(2):
                at = r * NBLK + 2 * cb + e
                pair.append(mbuf[inv_s[at // lanes, 0, lax.rem(at, lanes)], pl.ds(0, span), :])
            rows.append(jnp.concatenate(pair, axis=1))
        value = jnp.dot(lhs[...], jnp.concatenate(rows, axis=0), preferred_element_type=jnp.float32)
        out[:, pl.ds(pl.multiple_of(cb * 2 * lanes, 2 * lanes), 2 * lanes)] = value.astype(jnp.bfloat16)
        return carry
    lax.fori_loop(0, NBLK // 2, columns, 0)

    for c in range(CHUNKS):
        sent(fbuf[c].at[pl.ds(0, 3 * own)], ysend.at[c], yp.at[c, 0])
        sent(fbuf[c].at[pl.ds(0, NY * own)], ssend.at[c], sib.at[c])
        for u in range(SUBS):
            ref = sbuf.at[c, pl.ds(0, NAUX - 1), pl.ds(u * gl * 4, gl * 4)]
            sent(ref, asend.at[c, u], arecv.at[c, u])
    sent(mbuf.at[pl.ds(0, (NZ - 1) * half)], msend.at[0], msib.at[0])
    sent(mbuf.at[pl.ds(0, NZ * half)], msend.at[1], msib.at[0])
    sent(mbuf.at[pl.ds(0, NZ * half)], msend.at[2], msib.at[0])
    sent(mbuf.at[pl.ds(0, (NAUX - 1) * half)], msend.at[3], msib.at[0])
    sent(mbuf.at[pl.ds(0, NZ * half)], msend.at[4], msib.at[0])


def shards(factors, amplitudes, partners, metric_tiles, tile_pos):
    own, domain, aux_part = factors.shape
    npair = partners.shape[1]
    nt, span = metric_tiles.shape[0], metric_tiles.shape[1]
    norb = own * 2 * NY
    pw = aux_part // CHUNKS
    ng = own * pw // 128
    keys = (tile_pos[:, 0] * NBLK + tile_pos[:, 1]).astype(jnp.bfloat16)
    meta = jnp.broadcast_to(keys[:, None, None], (nt, 16, 128))
    dma = pltpu.SemaphoreType.DMA
    anywhere = pl.BlockSpec(memory_space=pl.ANY)
    rows = own * domain // NAUX
    result = pl.pallas_call(
        kernel,
        out_shape=jax.ShapeDtypeStruct((rows, aux_part * NAUX), jnp.bfloat16),
        in_specs=[anywhere, anywhere, pl.BlockSpec(memory_space=pltpu.SMEM), anywhere, anywhere],
        out_specs=pl.BlockSpec(memory_space=pltpu.VMEM),
        scratch_shapes=[pltpu.VMEM((norb, pw, domain), jnp.bfloat16)] * CHUNKS + [
            pltpu.VMEM(amplitudes.shape, jnp.bfloat16),
            pltpu.VMEM((NAUX * nt + 1, span + 16, span), jnp.bfloat16),
            pltpu.VMEM((NAUX, 4 * ng // SUBS, 128), jnp.float32),
            pltpu.VMEM((CHUNKS, NAUX, 4 * ng, 128), jnp.bfloat16),
            pltpu.VMEM((CHUNKS, NAUX, 4 * ng, 128), jnp.bfloat16),
            pltpu.VMEM((rows, aux_part * NAUX), jnp.bfloat16),
            pltpu.VMEM((2, 8, 128), jnp.int32),
            pltpu.SMEM((2, 8, 128), jnp.int32),
            dma((4 + CHUNKS,)),
            dma((CHUNKS,)),
            dma((CHUNKS,)),
            dma((CHUNKS, PIECES)),
            dma((CHUNKS, PIECES)),
            dma((CHUNKS, PIECES // 2)),
            dma((CHUNKS, PIECES // 2)),
            dma((CHUNKS,)),
            dma((5,)),
            dma((NZ // 2,)),
            dma((NZ // 2,)),
            dma((NZ,)),
            dma((NZ,)),
            dma((NZ,)),
            dma((1,)),
            dma((CHUNKS, SUBS)),
            dma((CHUNKS, SUBS)),
        ],
        compiler_params=pltpu.CompilerParams(
            collective_id=0, has_side_effects=True, vmem_limit_bytes=60 * 1024 * 1024),
    )(jnp.swapaxes(factors, 1, 2), amplitudes, partners.T, metric_tiles, meta)
    return result.reshape(own, rows // own, aux_part * NAUX)


def solution(mesh):
    in_specs = (
        P("orb", None, "aux"),
        P("orb", None, None, None),
        P("orb", None),
        P("aux", None, None),
        P("aux", None),
    )
    out_specs = P("orb", "aux", None)
    return jax.shard_map(shards, mesh=mesh, in_specs=in_specs, out_specs=out_specs, check_vma=False)
```

```python
import jax
import jax.numpy as jnp
from jax import lax
from jax.experimental import pallas as pl
from jax.experimental.pallas import tpu as pltpu
from jax.sharding import PartitionSpec as P

MESH = pl.DeviceIdType.MESH
NY, NX, NZ = 4, 4, 8
NAUX = NX * NZ
WIDTHS = (32, 32)
STARTS = (0, 32)
CHUNKS = len(WIDTHS)
PIECES = (4, 4)
SUBS = 3
NBLK = 16
LANES = 128
WAVES = NZ // 2 - 1
XPLUS = (0, 1, 2, 4)
XMINUS = (5, 6, 7, 3)


def kernel(ft, amp, part, tiles, pos, out, *scratch):
    fbuf, sbuf, rbuf, lhs = (scratch[n * CHUNKS:(n + 1) * CHUNKS] for n in range(4))
    (ampv, mbuf, stage, acc, inv_v, inv_s) = scratch[4 * CHUNKS:4 * CHUNKS + 6]
    (loc, ysend, ssend, yp, ym, y2p, y2m, sib,
     msend, rzp, rzm, rxp, rxm, rx2, msib, asend, arecv, wave) = scratch[4 * CHUNKS + 6:]

    o = lax.axis_index("orb")
    s = lax.axis_index("aux")
    y, h = o // 2, o % 2
    x, z = s // NZ, s % NZ
    own, npair = amp.shape[0], amp.shape[1]
    nt, span = tiles.shape[0], tiles.shape[1]
    half = nt // 2
    pers = [LANES // pw for pw in WIDTHS]
    groups = [own // per for per in pers]

    def orb_at(dy):
        return lax.rem(y + dy + NY, NY) * 2 + h

    def aux_at(dx, dz):
        return lax.rem(x + dx + NX, NX) * NZ + lax.rem(z + dz + NZ, NZ)

    columns_at = [lax.rem(x + dx, NX) * NZ for dx in range(NX)]
    sibling = (y * 2 + 1 - h, s)
    yplus, yminus = (orb_at(1), s), (orb_at(-1), s)
    xplus, xminus = (o, aux_at(1, 0)), (o, aux_at(-1, 0))
    zplus, zminus = (o, aux_at(0, 1)), (o, aux_at(0, -1))

    def remote(src, dst, ssem, rsem, dev):
        return pltpu.make_async_remote_copy(
            src_ref=src, dst_ref=dst, send_sem=ssem, recv_sem=rsem, device_id=dev, device_id_type=MESH)

    def recv(ref, ssem, rsem):
        remote(ref, ref, ssem, rsem, sibling).wait_recv()

    def sent(ref, ssem, rsem):
        remote(ref, ref, ssem, rsem, sibling).wait_send()

    def signal(sem, dev):
        pl.semaphore_signal(sem, inc=1, device_id=dev, device_id_type=MESH)

    barrier = pltpu.get_barrier_semaphore()
    for dev in (sibling, yplus, yminus, xplus, xminus, zplus, zminus):
        signal(barrier, dev)

    mine = pl.ds(s * nt, nt)
    load_tiles = pltpu.make_async_copy(tiles, mbuf.at[mine, pl.ds(0, span)], loc.at[0])
    load_tiles.start()
    for t in range(nt):
        key = (pos[0, t] * NBLK + pos[1, t]).astype(jnp.float32)
        mbuf[s * nt + t, pl.ds(span, 16), :] = jnp.full((16, LANES), key, jnp.float32).astype(jnp.bfloat16)
    mbuf[NAUX * nt] = jnp.zeros(mbuf.shape[1:], jnp.bfloat16)
    load_own = [
        pltpu.make_async_copy(
            ft.at[:, pl.ds(STARTS[c], WIDTHS[c]), :], fbuf[c].at[pl.ds(o * own, own)], loc.at[2 + c])
        for c in range(CHUNKS)
    ]
    load_amp = pltpu.make_async_copy(amp, ampv, loc.at[2 + CHUNKS])

    def fpiece(c, orb, q):
        npc = own // PIECES[c]
        return fbuf[c].at[pl.ds(orb * own + q * npc, npc)]

    def to_sibling(c, ref):
        remote(ref, ref, ssend.at[c], sib.at[c], sibling).start()

    def gather_start(c):
        npc = own // PIECES[c]
        for q in range(PIECES[c]):
            src = ft.at[pl.ds(q * npc, npc), pl.ds(STARTS[c], WIDTHS[c]), :]
            dst = fpiece(c, o, q)
            remote(src, dst, ysend.at[c], yp.at[c, q], yplus).start()
            remote(src, dst, ysend.at[c], ym.at[c, q], yminus).start()
        for q in range(PIECES[c]):
            src = ft.at[pl.ds(q * npc, npc), pl.ds(STARTS[c], WIDTHS[c]), :]
            remote(src, fpiece(c, o, q), ssend.at[c], sib.at[c], sibling).start()

    def gather_round(c, q):
        below, above = fpiece(c, orb_at(-1), q), fpiece(c, orb_at(1), q)
        mid = PIECES[c] // 2
        recv(below, ysend.at[c], yp.at[c, q])
        if q < mid:
            remote(below, below, ysend.at[c], y2p.at[c, q], yplus).start()
        to_sibling(c, below)
        recv(above, ysend.at[c], ym.at[c, q])
        if q >= mid:
            remote(above, above, ysend.at[c], y2m.at[c, q - mid], yminus).start()
        to_sibling(c, above)

    def gather_far(c, q):
        mid = PIECES[c] // 2
        low, high = fpiece(c, orb_at(2), q), fpiece(c, orb_at(2), q + mid)
        recv(low, ysend.at[c], y2p.at[c, q])
        to_sibling(c, low)
        recv(high, ysend.at[c], y2m.at[c, q])
        to_sibling(c, high)

    def gather_done(c):
        recv(fbuf[c].at[pl.ds(0, NY * own)], ssend.at[c], sib.at[c])
        load_own[c].wait()

    def shard(dx, idx):
        dz = -idx if idx <= NZ // 2 else idx - NZ // 2
        return mbuf.at[pl.ds(aux_at(dx, dz) * nt + h * half, half)]

    def tiles_out(idx):
        ref = shard(0, idx)
        if idx < NZ // 2:
            remote(ref, ref, msend.at[0], rzp.at[idx], zplus).start()
        if idx == 0:
            remote(ref, ref, msend.at[0], rzm.at[0], zminus).start()
        elif idx > NZ // 2 and idx < NZ - 1:
            remote(ref, ref, msend.at[0], rzm.at[idx - NZ // 2], zminus).start()
        remote(ref, ref, msend.at[1], rxp.at[idx], xplus).start()
        remote(ref, ref, msend.at[2], rxm.at[idx], xminus).start()
        if idx:
            remote(ref, ref, msend.at[3], msib.at[0], sibling).start()

    def tiles_x(idx):
        left, right = shard(-1, idx), shard(1, idx)
        recv(left, msend.at[1], rxp.at[idx])
        if idx in XPLUS:
            remote(left, left, msend.at[4], rx2.at[idx], xplus).start()
        remote(left, left, msend.at[3], msib.at[0], sibling).start()
        recv(right, msend.at[2], rxm.at[idx])
        if idx in XMINUS:
            remote(right, right, msend.at[4], rx2.at[idx], xminus).start()
        remote(right, right, msend.at[3], msib.at[0], sibling).start()

    def tiles_z(k):
        recv(shard(0, k), msend.at[0], rzp.at[k - 1])
        tiles_out(k)
        if k < NZ // 2:
            recv(shard(0, NZ // 2 + k), msend.at[0], rzm.at[k - 1])
            tiles_out(NZ // 2 + k)

    def tiles_far(idx):
        far = shard(2, idx)
        recv(far, msend.at[4], rx2.at[idx])
        remote(far, far, msend.at[3], msib.at[0], sibling).start()

    def tiles_done():
        recv(mbuf.at[pl.ds(0, (NAUX - 1) * half)], msend.at[3], msib.at[0])

    def wave_out(k):
        for dev in (zplus, zminus) if k < WAVES else (xplus, xminus):
            signal(wave.at[k], dev)

    def wave_next(k):
        pl.semaphore_wait(wave.at[k], 2)
        if k < WAVES + 1:
            wave_out(k + 1)

    def contract(c, g):
        pw, per, ng = WIDTHS[c], pers[c], groups[c]
        blank = {n: jnp.zeros((n * pw, LANES), jnp.bfloat16) for n in range(1, per)}
        left, right = [], []
        for k in range(npair):
            for q in range(per):
                i = q * ng + g
                left.append(ampv[i, k])
                rows = [fbuf[c][part[k, i]]]
                if q:
                    rows.insert(0, blank[q])
                if q < per - 1:
                    rows.append(blank[per - 1 - q])
                right.append(jnp.concatenate(rows, axis=0))
        return lax.dot_general(
            jnp.concatenate(left, axis=1), jnp.concatenate(right, axis=1),
            (((1,), (1,)), ((), ())), preferred_element_type=jnp.float32)

    def contract_part(c, u, events=()):
        gl = groups[c] // SUBS
        rows = pl.ds(0, gl * 4)
        for g in range(gl):
            value = contract(c, u * gl + g)
            for r in range(NAUX):
                stage[r, g * 4:g * 4 + 4, :] = value[4 * r:4 * r + 4, :]
            for event in events[g:g + 1]:
                event()

        def pack(r, carry):
            sbuf[c][u, r] = stage[r, rows, :].astype(jnp.bfloat16)
            return carry
        lax.fori_loop(0, NAUX, pack, 0, unroll=4)

        def put(to):
            remote(sbuf[c].at[u, to], rbuf[c].at[u, s], asend.at[c, u], arecv.at[c, u], (o, to)).start()

        def send(a, carry):
            dz = NZ // 2 + (1 - 2 * (a % 2)) * ((a + 1) // 2)
            there = lax.rem(z + dz, NZ)
            for dx in (2, 1, 3, 0):
                put(columns_at[dx] + there)
            return carry
        lax.fori_loop(0, NZ - 1, send, 0)
        for dx in (2, 1, 3):
            put(columns_at[dx] + z)
        rbuf[c][u, s] = sbuf[c][u, s]

    def look_up():
        def look(t, carry):
            low, high = carry
            key = mbuf[t, pl.ds(span, 16), :].astype(jnp.int32)
            lane = lax.broadcasted_iota(jnp.int32, key.shape, 1)
            return jnp.where(key == lane, t, low), jnp.where(key == lane + LANES, t, high)

        none = jnp.full((16, LANES), NAUX * nt, jnp.int32)
        low, high = lax.fori_loop(0, NAUX * nt, look, (none, none), unroll=8)
        inv_v[0] = low[0:8]
        inv_v[1] = high[0:8]
        copy = pltpu.make_async_copy(inv_v, inv_s, loc.at[1])
        copy.start()
        copy.wait()

    def arrange(c, u):
        pw, per, ng = WIDTHS[c], pers[c], groups[c]
        rows = 4 * ng // SUBS
        recv(rbuf[c].at[u, pl.ds(0, NAUX - 1)], asend.at[c, u], arecv.at[c, u])

        def body(b, carry):
            at = pl.multiple_of(b * LANES, LANES)
            blocks = [rbuf[c][u, b * per + e] for e in range(per)]
            for q in range(per):
                lhs[c][pl.ds((q * SUBS + u) * rows, rows), pl.ds(at, LANES)] = jnp.concatenate(
                    [blk[:, q * pw:(q + 1) * pw] for blk in blocks], axis=1)
            return carry
        lax.fori_loop(0, NAUX // per, body, 0, unroll=2)

    def product(cs, first, last):
        def columns(cb, carry):
            at = pl.ds(pl.multiple_of(cb * 2 * LANES, 2 * LANES), 2 * LANES)
            ids = [[inv_s[(r * NBLK + 2 * cb + e) // LANES, 0, lax.rem(r * NBLK + 2 * cb + e, LANES)]
                    for e in range(2)] for r in range(NBLK)]
            total = None if first else acc[:, at]
            for c in cs:
                rows = []
                for r in range(NBLK):
                    for e in range(2):
                        rows.append(jnp.concatenate(
                            [mbuf[ids[r][n], pl.ds(e * (span // 2) + STARTS[c], WIDTHS[c]), :] for n in range(2)],
                            axis=1))
                value = jnp.dot(lhs[c][...], jnp.concatenate(rows, axis=0), preferred_element_type=jnp.float32)
                total = value if total is None else total + value
            if last:
                out[:, at] = total.astype(jnp.bfloat16)
            else:
                acc[:, at] = total
            return carry
        lax.fori_loop(0, NBLK // 2, columns, 0, unroll=2)

    pl.semaphore_wait(barrier, 7)
    gather_start(0)
    wave_out(0)
    load_tiles.wait()
    tiles_out(0)
    for copy in load_own:
        copy.start()
    load_amp.start()

    def skip():
        pass

    def both(*events):
        def run():
            for event, *rest in events:
                event(*rest)
        return run

    for k in range(3):
        wave_next(k)
    gather_round(0, 0)
    wave_next(3)
    gather_round(0, 1)
    tiles_x(0)
    tiles_z(1)
    wave_next(4)
    gather_round(0, 2)
    gather_round(0, 3)
    gather_start(1)
    tiles_z(2)
    tiles_far(0)
    gather_far(0, 0)
    tiles_x(1)
    gather_far(0, 1)
    tiles_x(5)
    tiles_z(3)
    gather_done(0)
    load_amp.wait()
    contract_part(0, 0, [skip, both((gather_round, 1, 0)), skip, both((tiles_x, 2))])
    contract_part(0, 1, [both((gather_round, 1, 1)), both((tiles_z, 4)), both((tiles_x, 6)), skip])
    contract_part(0, 2, [both((tiles_far, 5)), both((tiles_far, 1)), both((gather_round, 1, 2)), skip])
    tiles_x(3)
    gather_round(1, 3)
    tiles_x(7)
    tiles_far(2)
    tiles_far(6)
    gather_far(1, 0)
    tiles_x(4)
    tiles_far(7)
    gather_far(1, 1)
    gather_done(1)
    contract_part(1, 0, [both((tiles_far, 3)), both((tiles_far, 4))])
    contract_part(1, 1)
    contract_part(1, 2)
    tiles_done()
    look_up()
    for u in range(SUBS):
        arrange(0, u)
    product((0,), True, False)
    for u in range(SUBS):
        arrange(1, u)
    product((1,), False, True)

    for c in range(CHUNKS):
        sent(fbuf[c].at[pl.ds(0, 3 * own)], ysend.at[c], yp.at[c, 0])
        sent(fbuf[c].at[pl.ds(0, NY * own)], ssend.at[c], sib.at[c])
        for u in range(SUBS):
            sent(sbuf[c].at[u, pl.ds(0, NAUX - 1)], asend.at[c, u], arecv.at[c, u])
    sent(mbuf.at[pl.ds(0, (NZ - 1) * half)], msend.at[0], msib.at[0])
    sent(mbuf.at[pl.ds(0, NZ * half)], msend.at[1], msib.at[0])
    sent(mbuf.at[pl.ds(0, NZ * half)], msend.at[2], msib.at[0])
    sent(mbuf.at[pl.ds(0, (NAUX - 1) * half)], msend.at[3], msib.at[0])
    sent(mbuf.at[pl.ds(0, NZ * half)], msend.at[4], msib.at[0])


def shards(factors, amplitudes, partners, metric_tiles, tile_pos):
    own, domain, aux_part = factors.shape
    nt, span = metric_tiles.shape[0], metric_tiles.shape[1]
    norb = own * 2 * NY
    rows = own * domain // NAUX
    dma = pltpu.SemaphoreType.DMA
    anywhere = pl.BlockSpec(memory_space=pl.ANY)
    scalars = pl.BlockSpec(memory_space=pltpu.SMEM)
    parts = [pltpu.VMEM((SUBS, NAUX, rows * pw // LANES // SUBS, LANES), jnp.bfloat16) for pw in WIDTHS]
    result = pl.pallas_call(
        kernel,
        out_shape=jax.ShapeDtypeStruct((rows, aux_part * NAUX), jnp.bfloat16),
        in_specs=[anywhere, anywhere, scalars, anywhere, scalars],
        out_specs=pl.BlockSpec(memory_space=pltpu.VMEM),
        scratch_shapes=[pltpu.VMEM((norb, pw, domain), jnp.bfloat16) for pw in WIDTHS] + parts + parts + [
            pltpu.VMEM((rows, pw * NAUX), jnp.bfloat16) for pw in WIDTHS] + [
            pltpu.VMEM(amplitudes.shape, jnp.bfloat16),
            pltpu.VMEM((NAUX * nt + 1, span + 16, span), jnp.bfloat16),
            pltpu.VMEM((NAUX, 16, LANES), jnp.float32),
            pltpu.VMEM((rows, aux_part * NAUX), jnp.float32),
            pltpu.VMEM((2, 8, LANES), jnp.int32),
            pltpu.SMEM((2, 8, LANES), jnp.int32),
            dma((3 + CHUNKS,)),
            dma((CHUNKS,)),
            dma((CHUNKS,)),
            dma((CHUNKS, max(PIECES))),
            dma((CHUNKS, max(PIECES))),
            dma((CHUNKS, max(PIECES) // 2)),
            dma((CHUNKS, max(PIECES) // 2)),
            dma((CHUNKS,)),
            dma((5,)),
            dma((NZ // 2,)),
            dma((NZ // 2,)),
            dma((NZ,)),
            dma((NZ,)),
            dma((NZ,)),
            dma((1,)),
            dma((CHUNKS, SUBS)),
            dma((CHUNKS, SUBS)),
            pltpu.SemaphoreType.REGULAR((WAVES + 2,)),
        ],
        compiler_params=pltpu.CompilerParams(
            collective_id=0, has_side_effects=True, vmem_limit_bytes=60 * 1024 * 1024),
    )(jnp.swapaxes(factors, 1, 2), amplitudes, partners.T, metric_tiles, tile_pos.T)
    return result.reshape(own, rows // own, aux_part * NAUX)


def solution(mesh):
    in_specs = (
        P("orb", None, "aux"),
        P("orb", None, None, None),
        P("orb", None),
        P("aux", None, None),
        P("aux", None),
    )
    out_specs = P("orb", "aux", None)
    return jax.shard_map(shards, mesh=mesh, in_specs=in_specs, out_specs=out_specs, check_vma=False)
```

```python
import jax
import jax.numpy as jnp
from jax import lax
from jax.experimental import pallas as pl
from jax.experimental.pallas import tpu as pltpu
from jax.sharding import PartitionSpec as P

MESH = pl.DeviceIdType.MESH
NY, NX, NZ = 4, 4, 8
NAUX = NX * NZ
WIDTHS = (32, 32)
STARTS = (0, 32)
CHUNKS = len(WIDTHS)
PIECES = (4, 4)
SUBS = 3
NBLK = 16
LANES = 128
WAVES = NZ // 2 - 1
XPLUS = (0, 1, 2, 4)
XMINUS = (5, 6, 7, 3)


def kernel(ft, amp, part_in, tiles, pos_in, result, *scratch):
    fbuf, sbuf, rbuf, lhs = (scratch[n * CHUNKS:(n + 1) * CHUNKS] for n in range(4))
    (ampv, mbuf, stage, acc, inv_v, inv_s, out, part, pos) = scratch[4 * CHUNKS:4 * CHUNKS + 9]
    (loc, ysend, ssend, yp, ym, y2p, y2m, sib,
     msend, rz, rxp, rxm, rx2, msib, asend, arecv, wave) = scratch[4 * CHUNKS + 9:]

    o = lax.axis_index("orb")
    s = lax.axis_index("aux")
    y, h = o // 2, o % 2
    x, z = s // NZ, s % NZ
    own, npair = amp.shape[0], amp.shape[1]
    nt, span = tiles.shape[0], tiles.shape[1]
    half = nt // 2
    pers = [LANES // pw for pw in WIDTHS]
    groups = [own // per for per in pers]

    def orb_at(dy):
        return lax.rem(y + dy + NY, NY) * 2 + h

    def aux_at(dx, dz):
        return lax.rem(x + dx + NX, NX) * NZ + lax.rem(z + dz + NZ, NZ)

    columns_at = [lax.rem(x + dx, NX) * NZ for dx in range(NX)]
    sibling = (y * 2 + 1 - h, s)
    yplus, yminus = (orb_at(1), s), (orb_at(-1), s)
    xplus, xminus = (o, aux_at(1, 0)), (o, aux_at(-1, 0))
    zplus, zminus = (o, aux_at(0, 1)), (o, aux_at(0, -1))

    def remote(src, dst, ssem, rsem, dev):
        return pltpu.make_async_remote_copy(
            src_ref=src, dst_ref=dst, send_sem=ssem, recv_sem=rsem, device_id=dev, device_id_type=MESH)

    def recv(ref, ssem, rsem):
        remote(ref, ref, ssem, rsem, sibling).wait_recv()

    def sent(ref, ssem, rsem):
        remote(ref, ref, ssem, rsem, sibling).wait_send()

    def signal(sem, dev):
        pl.semaphore_signal(sem, inc=1, device_id=dev, device_id_type=MESH)

    barrier = pltpu.get_barrier_semaphore()
    for dev in (sibling, yplus, yminus, xplus, xminus, zplus, zminus):
        signal(barrier, dev)

    mine = pl.ds(s * nt, nt)
    load_tiles = pltpu.make_async_copy(tiles, mbuf.at[mine, pl.ds(0, span)], loc.at[0])
    load_tiles.start()
    load_pos = pltpu.make_async_copy(pos_in, pos, loc.at[3 + CHUNKS])
    load_pos.start()
    load_part = pltpu.make_async_copy(part_in, part, loc.at[4 + CHUNKS])
    load_part.start()
    load_pos.wait()
    for t in range(nt):
        key = (pos[0, t] * NBLK + pos[1, t]).astype(jnp.float32)
        mbuf[s * nt + t, pl.ds(span, 16), :] = jnp.full((16, LANES), key, jnp.float32).astype(jnp.bfloat16)
    mbuf[NAUX * nt] = jnp.zeros(mbuf.shape[1:], jnp.bfloat16)
    load_own = [
        pltpu.make_async_copy(
            ft.at[:, pl.ds(STARTS[c], WIDTHS[c]), :], fbuf[c].at[pl.ds(o * own, own)], loc.at[2 + c])
        for c in range(CHUNKS)
    ]
    load_amp = pltpu.make_async_copy(amp, ampv, loc.at[2 + CHUNKS])

    def fpiece(c, orb, q):
        npc = own // PIECES[c]
        return fbuf[c].at[pl.ds(orb * own + q * npc, npc)]

    def to_sibling(c, ref):
        remote(ref, ref, ssend.at[c], sib.at[c], sibling).start()

    def gather_start(c):
        npc = own // PIECES[c]
        mid = PIECES[c] // 2

        def put(q, ssem, rsem, dev):
            src = ft.at[pl.ds(q * npc, npc), pl.ds(STARTS[c], WIDTHS[c]), :]
            remote(src, fpiece(c, o, q), ssem, rsem, dev).start()
        for q in range(PIECES[c]):
            below = (q + mid) % PIECES[c]
            put(q, ysend.at[c], yp.at[c, q], yplus)
            put(below, ysend.at[c], ym.at[c, below], yminus)
        for q in range(PIECES[c]):
            put(q, ssend.at[c], sib.at[c], sibling)

    def gather_round(c, q):
        mid = PIECES[c] // 2
        high = (q + mid) % PIECES[c]
        below, above = fpiece(c, orb_at(-1), q), fpiece(c, orb_at(1), high)
        recv(below, ysend.at[c], yp.at[c, q])
        if q < mid:
            remote(below, below, ysend.at[c], y2p.at[c, q], yplus).start()
        to_sibling(c, below)
        recv(above, ysend.at[c], ym.at[c, high])
        if q < mid:
            remote(above, above, ysend.at[c], y2m.at[c, q], yminus).start()
        to_sibling(c, above)

    def gather_far(c, q):
        mid = PIECES[c] // 2
        low, high = fpiece(c, orb_at(2), q), fpiece(c, orb_at(2), q + mid)
        recv(low, ysend.at[c], y2p.at[c, q])
        to_sibling(c, low)
        recv(high, ysend.at[c], y2m.at[c, q])
        to_sibling(c, high)

    def gather_done(c):
        recv(fbuf[c].at[pl.ds(0, NY * own)], ssend.at[c], sib.at[c])
        load_own[c].wait()

    def shard(dx, idx):
        dz = -idx if idx <= NZ // 2 else idx - NZ // 2
        return mbuf.at[pl.ds(aux_at(dx, dz) * nt + h * half, half)]

    def tiles_x_out(idx):
        ref = shard(0, idx)
        remote(ref, ref, msend.at[1], rxp.at[idx], xplus).start()
        remote(ref, ref, msend.at[2], rxm.at[idx], xminus).start()

    def tiles_z_out():
        ref = shard(0, 0)
        for k in range(1, NZ // 2 + 1):
            remote(ref, ref, msend.at[0], rz.at[k], (o, aux_at(0, k))).start()
            if k < NZ // 2:
                remote(ref, ref, msend.at[0], rz.at[NZ // 2 + k], (o, aux_at(0, -k))).start()

    def tiles_z(idx):
        ref = shard(0, idx)
        recv(ref, msend.at[0], rz.at[idx])
        tiles_x_out(idx)
        remote(ref, ref, msend.at[3], msib.at[0], sibling).start()

    def tiles_x(idx):
        left, right = shard(-1, idx), shard(1, idx)
        recv(left, msend.at[1], rxp.at[idx])
        if idx in XPLUS:
            remote(left, left, msend.at[4], rx2.at[idx], xplus).start()
        remote(left, left, msend.at[3], msib.at[0], sibling).start()
        recv(right, msend.at[2], rxm.at[idx])
        if idx in XMINUS:
            remote(right, right, msend.at[4], rx2.at[idx], xminus).start()
        remote(right, right, msend.at[3], msib.at[0], sibling).start()

    def tiles_far(idx):
        far = shard(2, idx)
        recv(far, msend.at[4], rx2.at[idx])
        remote(far, far, msend.at[3], msib.at[0], sibling).start()

    def tiles_done():
        recv(mbuf.at[pl.ds(0, (NAUX - 1) * half)], msend.at[3], msib.at[0])

    def wave_out(k):
        for dev in (zplus, zminus) if k < WAVES else (xplus, xminus):
            signal(wave.at[k], dev)

    def wave_next(k):
        pl.semaphore_wait(wave.at[k], 2)
        if k < WAVES + 1:
            wave_out(k + 1)

    def contract(c, g):
        pw, per, ng = WIDTHS[c], pers[c], groups[c]
        blank = {n: jnp.zeros((n * pw, LANES), jnp.bfloat16) for n in range(1, per)}
        left, right = [], []
        for k in range(npair):
            for q in range(per):
                i = q * ng + g
                left.append(ampv[i, k])
                rows = [fbuf[c][part[k, i]]]
                if q:
                    rows.insert(0, blank[q])
                if q < per - 1:
                    rows.append(blank[per - 1 - q])
                right.append(jnp.concatenate(rows, axis=0))
        return lax.dot_general(
            jnp.concatenate(left, axis=1), jnp.concatenate(right, axis=1),
            (((1,), (1,)), ((), ())), preferred_element_type=jnp.float32)

    def contract_part(c, u, events=()):
        gl = groups[c] // SUBS
        rows = pl.ds(0, gl * 4)
        for g in range(gl):
            value = contract(c, u * gl + g)
            for r in range(NAUX):
                stage[r, g * 4:g * 4 + 4, :] = value[4 * r:4 * r + 4, :]
            for event in events[g:g + 1]:
                event()

        def pack(r, carry):
            sbuf[c][u, r] = stage[r, rows, :].astype(jnp.bfloat16)
            return carry
        lax.fori_loop(0, NAUX, pack, 0, unroll=4)

        def put(to):
            remote(sbuf[c].at[u, to], rbuf[c].at[u, s], asend.at[c, u], arecv.at[c, u], (o, to)).start()

        def send(a, carry):
            dz = NZ // 2 + (1 - 2 * (a % 2)) * ((a + 1) // 2)
            there = lax.rem(z + dz, NZ)
            for dx in (2, 1, 3, 0):
                put(columns_at[dx] + there)
            return carry
        lax.fori_loop(0, NZ - 1, send, 0)
        for dx in (2, 1, 3):
            put(columns_at[dx] + z)
        rbuf[c][u, s] = sbuf[c][u, s]

    def look_up():
        def look(t, carry):
            low, high = carry
            key = mbuf[t, pl.ds(span, 16), :].astype(jnp.int32)
            lane = lax.broadcasted_iota(jnp.int32, key.shape, 1)
            return jnp.where(key == lane, t, low), jnp.where(key == lane + LANES, t, high)

        none = jnp.full((16, LANES), NAUX * nt, jnp.int32)
        low, high = lax.fori_loop(0, NAUX * nt, look, (none, none), unroll=8)
        inv_v[0] = low[0:8]
        inv_v[1] = high[0:8]
        copy = pltpu.make_async_copy(inv_v, inv_s, loc.at[1])
        copy.start()
        copy.wait()

    def arrange(c, u):
        pw, per, ng = WIDTHS[c], pers[c], groups[c]
        rows = 4 * ng // SUBS
        recv(rbuf[c].at[u, pl.ds(0, NAUX - 1)], asend.at[c, u], arecv.at[c, u])

        def body(b, carry):
            at = pl.multiple_of(b * LANES, LANES)
            blocks = [rbuf[c][u, b * per + e] for e in range(per)]
            for q in range(per):
                lhs[c][pl.ds((q * SUBS + u) * rows, rows), pl.ds(at, LANES)] = jnp.concatenate(
                    [blk[:, q * pw:(q + 1) * pw] for blk in blocks], axis=1)
            return carry
        lax.fori_loop(0, NAUX // per, body, 0, unroll=2)

    def product(cs, first, last):
        def columns(cb, carry):
            at = pl.ds(pl.multiple_of(cb * 2 * LANES, 2 * LANES), 2 * LANES)
            ids = [[inv_s[(r * NBLK + 2 * cb + e) // LANES, 0, lax.rem(r * NBLK + 2 * cb + e, LANES)]
                    for e in range(2)] for r in range(NBLK)]
            total = None if first else acc[:, at]
            for c in cs:
                rows = []
                for r in range(NBLK):
                    for e in range(2):
                        rows.append(jnp.concatenate(
                            [mbuf[ids[r][n], pl.ds(e * (span // 2) + STARTS[c], WIDTHS[c]), :] for n in range(2)],
                            axis=1))
                value = jnp.dot(lhs[c][...], jnp.concatenate(rows, axis=0), preferred_element_type=jnp.float32)
                total = value if total is None else total + value
            if last:
                out[:, at] = total.astype(jnp.bfloat16)
                pltpu.make_async_copy(out.at[:, at], result.at[:, at], loc.at[5 + CHUNKS]).start()
            else:
                acc[:, at] = total
            return carry
        lax.fori_loop(0, NBLK // 2, columns, 0, unroll=2)

    pl.semaphore_wait(barrier, 7)
    gather_start(0)
    wave_out(0)
    load_tiles.wait()
    tiles_x_out(0)
    for copy in load_own:
        copy.start()
    load_amp.start()

    def skip():
        pass

    def both(*events):
        def run():
            for event, *rest in events:
                event(*rest)
        return run

    for k in range(WAVES):
        wave_next(k)
    tiles_z_out()
    wave_next(3)
    gather_round(0, 0)
    wave_next(4)
    gather_round(0, 1)
    gather_start(1)
    tiles_x(0)
    tiles_z(1)
    tiles_z(5)
    tiles_far(0)
    tiles_z(2)
    gather_round(0, 2)
    tiles_z(6)
    tiles_x(1)
    tiles_x(5)
    gather_round(0, 3)
    tiles_z(3)
    tiles_z(7)
    gather_far(0, 0)
    tiles_x(2)
    tiles_z(4)
    gather_far(0, 1)
    gather_done(0)
    load_amp.wait()
    load_part.wait()
    contract_part(0, 0, [skip, both((gather_round, 1, 0)), both((tiles_x, 6)), both((tiles_far, 5), (tiles_far, 1))])
    contract_part(0, 1, [both((gather_round, 1, 1)), both((tiles_x, 3)), both((tiles_x, 7)), skip])
    contract_part(0, 2, [both((tiles_far, 6)), both((tiles_far, 2)), skip, both((gather_round, 1, 2))])
    gather_round(1, 3)
    tiles_x(4)
    tiles_far(7)
    gather_far(1, 0)
    gather_far(1, 1)
    gather_done(1)
    contract_part(1, 0, [skip, skip, skip, both((tiles_far, 3), (tiles_far, 4))])
    contract_part(1, 1)
    contract_part(1, 2)
    tiles_done()
    look_up()
    for u in range(SUBS):
        arrange(0, u)
    product((0,), True, False)
    for u in range(SUBS):
        arrange(1, u)
    product((1,), False, True)

    pltpu.make_async_copy(out, result, loc.at[5 + CHUNKS]).wait()
    for c in range(CHUNKS):
        sent(fbuf[c].at[pl.ds(0, 3 * own)], ysend.at[c], yp.at[c, 0])
        sent(fbuf[c].at[pl.ds(0, NY * own)], ssend.at[c], sib.at[c])
        for u in range(SUBS):
            sent(sbuf[c].at[u, pl.ds(0, NAUX - 1)], asend.at[c, u], arecv.at[c, u])
    sent(mbuf.at[pl.ds(0, (NZ - 1) * half)], msend.at[0], msib.at[0])
    sent(mbuf.at[pl.ds(0, NZ * half)], msend.at[1], msib.at[0])
    sent(mbuf.at[pl.ds(0, NZ * half)], msend.at[2], msib.at[0])
    sent(mbuf.at[pl.ds(0, (NAUX - 1) * half)], msend.at[3], msib.at[0])
    sent(mbuf.at[pl.ds(0, NZ * half)], msend.at[4], msib.at[0])


def shards(factors, amplitudes, partners, metric_tiles, tile_pos):
    own, domain, aux_part = factors.shape
    nt, span = metric_tiles.shape[0], metric_tiles.shape[1]
    norb = own * 2 * NY
    rows = own * domain // NAUX
    dma = pltpu.SemaphoreType.DMA
    anywhere = pl.BlockSpec(memory_space=pl.ANY)
    parts = [pltpu.VMEM((SUBS, NAUX, rows * pw // LANES // SUBS, LANES), jnp.bfloat16) for pw in WIDTHS]
    result = pl.pallas_call(
        kernel,
        out_shape=jax.ShapeDtypeStruct((rows, aux_part * NAUX), jnp.bfloat16),
        in_specs=[anywhere] * 5,
        out_specs=anywhere,
        scratch_shapes=[pltpu.VMEM((norb, pw, domain), jnp.bfloat16) for pw in WIDTHS] + parts + parts + [
            pltpu.VMEM((rows, pw * NAUX), jnp.bfloat16) for pw in WIDTHS] + [
            pltpu.VMEM(amplitudes.shape, jnp.bfloat16),
            pltpu.VMEM((NAUX * nt + 1, span + 16, span), jnp.bfloat16),
            pltpu.VMEM((NAUX, 16, LANES), jnp.float32),
            pltpu.VMEM((rows, aux_part * NAUX), jnp.float32),
            pltpu.VMEM((2, 8, LANES), jnp.int32),
            pltpu.SMEM((2, 8, LANES), jnp.int32),
            pltpu.VMEM((rows, aux_part * NAUX), jnp.bfloat16),
            pltpu.SMEM(partners.shape[::-1], jnp.int32),
            pltpu.SMEM(tile_pos.shape[::-1], jnp.int32),
            dma((6 + CHUNKS,)),
            dma((CHUNKS,)),
            dma((CHUNKS,)),
            dma((CHUNKS, max(PIECES))),
            dma((CHUNKS, max(PIECES))),
            dma((CHUNKS, max(PIECES) // 2)),
            dma((CHUNKS, max(PIECES) // 2)),
            dma((CHUNKS,)),
            dma((5,)),
            dma((NZ,)),
            dma((NZ,)),
            dma((NZ,)),
            dma((NZ,)),
            dma((1,)),
            dma((CHUNKS, SUBS)),
            dma((CHUNKS, SUBS)),
            pltpu.SemaphoreType.REGULAR((WAVES + 2,)),
        ],
        compiler_params=pltpu.CompilerParams(
            collective_id=0, has_side_effects=True, vmem_limit_bytes=60 * 1024 * 1024),
    )(jnp.swapaxes(factors, 1, 2), amplitudes, partners.T, metric_tiles, tile_pos.T)
    return result.reshape(own, rows // own, aux_part * NAUX)


def solution(mesh):
    in_specs = (
        P("orb", None, "aux"),
        P("orb", None, None, None),
        P("orb", None),
        P("aux", None, None),
        P("aux", None),
    )
    out_specs = P("orb", "aux", None)
    return jax.shard_map(shards, mesh=mesh, in_specs=in_specs, out_specs=out_specs, check_vma=False)
```

```python
import jax
import jax.numpy as jnp
from jax import lax
from jax.experimental import pallas as pl
from jax.experimental.pallas import tpu as pltpu
from jax.sharding import PartitionSpec as P

MESH = pl.DeviceIdType.MESH
NY, NX, NZ = 4, 4, 8
NAUX = NX * NZ
WIDTHS = (32, 32)
STARTS = (0, 32)
CHUNKS = len(WIDTHS)
PIECES = (4, 4)
SUBS = 3
NBLK = 16
LANES = 128
WAVES = NZ // 2 - 1
XPLUS = (0, 1, 2, 4)
XMINUS = (5, 6, 7, 3)


def kernel(ft, amp, part_in, tiles, pos_in, result, *scratch):
    fbuf, sbuf, rbuf, lhs = (scratch[n * CHUNKS:(n + 1) * CHUNKS] for n in range(4))
    (ampv, mbuf, stage, acc, inv_v, inv_s, out, part, pos) = scratch[4 * CHUNKS:4 * CHUNKS + 9]
    (loc, ysend, ssend, yp, ym, y2p, y2m, sib,
     msend, rz, rxp, rxm, rx2, msib, asend, arecv, wave) = scratch[4 * CHUNKS + 9:]

    o = lax.axis_index("orb")
    s = lax.axis_index("aux")
    y, h = o // 2, o % 2
    x, z = s // NZ, s % NZ
    own, npair = amp.shape[0], amp.shape[1]
    nt, span = tiles.shape[0], tiles.shape[1]
    half = nt // 2
    pers = [LANES // pw for pw in WIDTHS]
    groups = [own // per for per in pers]

    def orb_at(dy):
        return lax.rem(y + dy + NY, NY) * 2 + h

    def aux_at(dx, dz):
        return lax.rem(x + dx + NX, NX) * NZ + lax.rem(z + dz + NZ, NZ)

    columns_at = [lax.rem(x + dx, NX) * NZ for dx in range(NX)]
    sibling = (y * 2 + 1 - h, s)
    yplus, yminus = (orb_at(1), s), (orb_at(-1), s)
    xplus, xminus = (o, aux_at(1, 0)), (o, aux_at(-1, 0))
    zplus, zminus = (o, aux_at(0, 1)), (o, aux_at(0, -1))

    def remote(src, dst, ssem, rsem, dev):
        return pltpu.make_async_remote_copy(
            src_ref=src, dst_ref=dst, send_sem=ssem, recv_sem=rsem, device_id=dev, device_id_type=MESH)

    def recv(ref, ssem, rsem):
        remote(ref, ref, ssem, rsem, sibling).wait_recv()

    def sent(ref, ssem, rsem):
        remote(ref, ref, ssem, rsem, sibling).wait_send()

    def signal(sem, dev):
        pl.semaphore_signal(sem, inc=1, device_id=dev, device_id_type=MESH)

    barrier = pltpu.get_barrier_semaphore()
    for dev in (sibling, yplus, yminus, xplus, xminus, zplus, zminus):
        signal(barrier, dev)

    mine = pl.ds(s * nt, nt)
    load_tiles = pltpu.make_async_copy(tiles, mbuf.at[mine, pl.ds(0, span)], loc.at[0])
    load_tiles.start()
    load_pos = pltpu.make_async_copy(pos_in, pos, loc.at[3 + CHUNKS])
    load_pos.start()
    load_part = pltpu.make_async_copy(part_in, part, loc.at[4 + CHUNKS])
    load_part.start()
    load_pos.wait()
    for t in range(nt):
        key = (pos[0, t] * NBLK + pos[1, t]).astype(jnp.float32)
        mbuf[s * nt + t, pl.ds(span, 16), :] = jnp.full((16, LANES), key, jnp.float32).astype(jnp.bfloat16)
    mbuf[NAUX * nt] = jnp.zeros(mbuf.shape[1:], jnp.bfloat16)
    load_own = [
        pltpu.make_async_copy(
            ft.at[:, pl.ds(STARTS[c], WIDTHS[c]), :], fbuf[c].at[pl.ds(o * own, own)], loc.at[2 + c])
        for c in range(CHUNKS)
    ]
    load_amp = pltpu.make_async_copy(amp, ampv, loc.at[2 + CHUNKS])

    def fpiece(c, orb, q):
        npc = own // PIECES[c]
        return fbuf[c].at[pl.ds(orb * own + q * npc, npc)]

    def to_sibling(c, ref):
        remote(ref, ref, ssend.at[c], sib.at[c], sibling).start()

    def gather_start(c):
        npc = own // PIECES[c]
        mid = PIECES[c] // 2

        def put(q, ssem, rsem, dev):
            src = ft.at[pl.ds(q * npc, npc), pl.ds(STARTS[c], WIDTHS[c]), :]
            remote(src, fpiece(c, o, q), ssem, rsem, dev).start()
        for q in range(PIECES[c]):
            below = (q + mid) % PIECES[c]
            put(q, ysend.at[c], yp.at[c, q], yplus)
            put(below, ysend.at[c], ym.at[c, below], yminus)
        for q in range(PIECES[c]):
            put(q, ssend.at[c], sib.at[c], sibling)

    def gather_round(c, q):
        mid = PIECES[c] // 2
        high = (q + mid) % PIECES[c]
        below, above = fpiece(c, orb_at(-1), q), fpiece(c, orb_at(1), high)
        recv(below, ysend.at[c], yp.at[c, q])
        if q < mid:
            remote(below, below, ysend.at[c], y2p.at[c, q], yplus).start()
        to_sibling(c, below)
        recv(above, ysend.at[c], ym.at[c, high])
        if q < mid:
            remote(above, above, ysend.at[c], y2m.at[c, q], yminus).start()
        to_sibling(c, above)

    def gather_far(c, q):
        mid = PIECES[c] // 2
        low, high = fpiece(c, orb_at(2), q), fpiece(c, orb_at(2), q + mid)
        recv(low, ysend.at[c], y2p.at[c, q])
        to_sibling(c, low)
        recv(high, ysend.at[c], y2m.at[c, q])
        to_sibling(c, high)

    def gather_done(c):
        recv(fbuf[c].at[pl.ds(0, NY * own)], ssend.at[c], sib.at[c])
        load_own[c].wait()

    def shard(dx, idx):
        dz = -idx if idx <= NZ // 2 else idx - NZ // 2
        return mbuf.at[pl.ds(aux_at(dx, dz) * nt + h * half, half)]

    def tiles_x_out(idx):
        ref = shard(0, idx)
        remote(ref, ref, msend.at[1], rxp.at[idx], xplus).start()
        remote(ref, ref, msend.at[2], rxm.at[idx], xminus).start()

    def tiles_z_out():
        ref = shard(0, 0)
        for k in range(1, NZ // 2 + 1):
            remote(ref, ref, msend.at[0], rz.at[k], (o, aux_at(0, k))).start()
            if k < NZ // 2:
                remote(ref, ref, msend.at[0], rz.at[NZ // 2 + k], (o, aux_at(0, -k))).start()

    def tiles_z(idx):
        ref = shard(0, idx)
        recv(ref, msend.at[0], rz.at[idx])
        tiles_x_out(idx)
        remote(ref, ref, msend.at[3], msib.at[0], sibling).start()

    def tiles_x(idx):
        left, right = shard(-1, idx), shard(1, idx)
        recv(left, msend.at[1], rxp.at[idx])
        if idx in XPLUS:
            remote(left, left, msend.at[4], rx2.at[idx], xplus).start()
        remote(left, left, msend.at[3], msib.at[0], sibling).start()
        recv(right, msend.at[2], rxm.at[idx])
        if idx in XMINUS:
            remote(right, right, msend.at[4], rx2.at[idx], xminus).start()
        remote(right, right, msend.at[3], msib.at[0], sibling).start()

    def tiles_far(idx):
        far = shard(2, idx)
        recv(far, msend.at[4], rx2.at[idx])
        remote(far, far, msend.at[3], msib.at[0], sibling).start()

    def tiles_done():
        recv(mbuf.at[pl.ds(0, (NAUX - 1) * half)], msend.at[3], msib.at[0])

    def wave_out(k):
        for dev in (zplus, zminus) if k < WAVES else (xplus, xminus):
            signal(wave.at[k], dev)

    def wave_next(k):
        pl.semaphore_wait(wave.at[k], 2)
        if k < WAVES + 1:
            wave_out(k + 1)

    def contract(c, g):
        pw, per, ng = WIDTHS[c], pers[c], groups[c]
        blank = {n: jnp.zeros((n * pw, LANES), jnp.bfloat16) for n in range(1, per)}
        left, right = [], []
        for k in range(npair):
            for q in range(per):
                i = q * ng + g
                left.append(ampv[i, k])
                rows = [fbuf[c][part[k, i]]]
                if q:
                    rows.insert(0, blank[q])
                if q < per - 1:
                    rows.append(blank[per - 1 - q])
                right.append(jnp.concatenate(rows, axis=0))
        return lax.dot_general(
            jnp.concatenate(left, axis=1), jnp.concatenate(right, axis=1),
            (((1,), (1,)), ((), ())), preferred_element_type=jnp.float32)

    def contract_part(c, u, events=()):
        gl = groups[c] // SUBS
        rows = pl.ds(0, gl * 4)
        for g in range(gl):
            value = contract(c, u * gl + g)
            for r in range(NAUX):
                stage[r, g * 4:g * 4 + 4, :] = value[4 * r:4 * r + 4, :]
            for event in events[g:g + 1]:
                event()

        def pack(r, carry):
            sbuf[c][u, r] = stage[r, rows, :].astype(jnp.bfloat16)
            return carry
        lax.fori_loop(0, NAUX, pack, 0, unroll=4)

        def put(to):
            remote(sbuf[c].at[u, to], rbuf[c].at[u, s], asend.at[c, u], arecv.at[c, u], (o, to)).start()

        def send(a, carry):
            dz = NZ // 2 + (1 - 2 * (a % 2)) * ((a + 1) // 2)
            there = lax.rem(z + dz, NZ)
            for dx in (2, 1, 3, 0):
                put(columns_at[dx] + there)
            return carry
        lax.fori_loop(0, NZ - 1, send, 0)
        for dx in (2, 1, 3):
            put(columns_at[dx] + z)
        rbuf[c][u, s] = sbuf[c][u, s]

    def look_up():
        def look(t, carry):
            low, high = carry
            key = mbuf[t, pl.ds(span, 16), :].astype(jnp.int32)
            lane = lax.broadcasted_iota(jnp.int32, key.shape, 1)
            return jnp.where(key == lane, t, low), jnp.where(key == lane + LANES, t, high)

        none = jnp.full((16, LANES), NAUX * nt, jnp.int32)
        low, high = lax.fori_loop(0, NAUX * nt, look, (none, none), unroll=8)
        inv_v[0] = low[0:8]
        inv_v[1] = high[0:8]
        copy = pltpu.make_async_copy(inv_v, inv_s, loc.at[1])
        copy.start()
        copy.wait()

    def arrange(c, u):
        pw, per, ng = WIDTHS[c], pers[c], groups[c]
        rows = 4 * ng // SUBS
        recv(rbuf[c].at[u, pl.ds(0, NAUX - 1)], asend.at[c, u], arecv.at[c, u])

        def body(b, carry):
            at = pl.multiple_of(b * LANES, LANES)
            blocks = [rbuf[c][u, b * per + e] for e in range(per)]
            for q in range(per):
                lhs[c][pl.ds((q * SUBS + u) * rows, rows), pl.ds(at, LANES)] = jnp.concatenate(
                    [blk[:, q * pw:(q + 1) * pw] for blk in blocks], axis=1)
            return carry
        lax.fori_loop(0, NAUX // per, body, 0, unroll=2)

    def product(cs, first, last):
        def columns(cb, carry):
            at = pl.ds(pl.multiple_of(cb * 2 * LANES, 2 * LANES), 2 * LANES)
            ids = [[inv_s[(r * NBLK + 2 * cb + e) // LANES, 0, lax.rem(r * NBLK + 2 * cb + e, LANES)]
                    for e in range(2)] for r in range(NBLK)]
            total = None if first else acc[:, at]
            for c in cs:
                rows = []
                for r in range(NBLK):
                    for e in range(2):
                        rows.append(jnp.concatenate(
                            [mbuf[ids[r][n], pl.ds(e * (span // 2) + STARTS[c], WIDTHS[c]), :] for n in range(2)],
                            axis=1))
                value = jnp.dot(lhs[c][...], jnp.concatenate(rows, axis=0), preferred_element_type=jnp.float32)
                total = value if total is None else total + value
            if last:
                out[:, at] = total.astype(jnp.bfloat16)
                pltpu.make_async_copy(out.at[:, at], result.at[:, at], loc.at[5 + CHUNKS]).start()
            else:
                acc[:, at] = total
            return carry
        lax.fori_loop(0, NBLK // 2, columns, 0, unroll=2)

    pl.semaphore_wait(barrier, 7)
    gather_start(0)
    wave_out(0)
    load_tiles.wait()
    tiles_x_out(0)
    for copy in load_own:
        copy.start()
    load_amp.start()

    def skip():
        pass

    def both(*events):
        def run():
            for event, *rest in events:
                event(*rest)
        return run

    for k in range(WAVES):
        wave_next(k)
    tiles_z_out()
    wave_next(3)
    gather_round(0, 0)
    wave_next(4)
    gather_round(0, 1)
    gather_start(1)
    tiles_x(0)
    tiles_z(1)
    tiles_z(5)
    tiles_far(0)
    tiles_z(2)
    gather_round(0, 2)
    tiles_z(6)
    tiles_x(1)
    tiles_x(5)
    gather_round(0, 3)
    tiles_z(3)
    tiles_z(7)
    gather_far(0, 0)
    tiles_x(2)
    tiles_z(4)
    gather_far(0, 1)
    gather_done(0)
    load_amp.wait()
    load_part.wait()
    contract_part(0, 0, [skip, both((gather_round, 1, 0)), skip, both((gather_round, 1, 1))])
    contract_part(0, 1, [both((tiles_x, 6)), both((tiles_far, 5), (tiles_far, 1)), skip, skip])
    contract_part(0, 2, [both((tiles_x, 3)), both((gather_round, 1, 2)), skip, skip])
    gather_round(1, 3)
    tiles_x(7)
    tiles_far(6)
    tiles_far(2)
    gather_far(1, 0)
    gather_far(1, 1)
    gather_done(1)
    contract_part(1, 0, [skip, skip, skip, both((tiles_x, 4), (tiles_far, 7))])
    contract_part(1, 1, [skip, skip, skip, both((tiles_far, 3), (tiles_far, 4))])
    contract_part(1, 2)
    tiles_done()
    look_up()
    for u in range(SUBS):
        arrange(0, u)
    product((0,), True, False)
    for u in range(SUBS):
        arrange(1, u)
    product((1,), False, True)

    pltpu.make_async_copy(out, result, loc.at[5 + CHUNKS]).wait()
    for c in range(CHUNKS):
        sent(fbuf[c].at[pl.ds(0, 3 * own)], ysend.at[c], yp.at[c, 0])
        sent(fbuf[c].at[pl.ds(0, NY * own)], ssend.at[c], sib.at[c])
        for u in range(SUBS):
            sent(sbuf[c].at[u, pl.ds(0, NAUX - 1)], asend.at[c, u], arecv.at[c, u])
    sent(mbuf.at[pl.ds(0, (NZ - 1) * half)], msend.at[0], msib.at[0])
    sent(mbuf.at[pl.ds(0, NZ * half)], msend.at[1], msib.at[0])
    sent(mbuf.at[pl.ds(0, NZ * half)], msend.at[2], msib.at[0])
    sent(mbuf.at[pl.ds(0, (NAUX - 1) * half)], msend.at[3], msib.at[0])
    sent(mbuf.at[pl.ds(0, NZ * half)], msend.at[4], msib.at[0])


def shards(factors, amplitudes, partners, metric_tiles, tile_pos):
    own, domain, aux_part = factors.shape
    nt, span = metric_tiles.shape[0], metric_tiles.shape[1]
    norb = own * 2 * NY
    rows = own * domain // NAUX
    dma = pltpu.SemaphoreType.DMA
    anywhere = pl.BlockSpec(memory_space=pl.ANY)
    parts = [pltpu.VMEM((SUBS, NAUX, rows * pw // LANES // SUBS, LANES), jnp.bfloat16) for pw in WIDTHS]
    result = pl.pallas_call(
        kernel,
        out_shape=jax.ShapeDtypeStruct((rows, aux_part * NAUX), jnp.bfloat16),
        in_specs=[anywhere] * 5,
        out_specs=anywhere,
        scratch_shapes=[pltpu.VMEM((norb, pw, domain), jnp.bfloat16) for pw in WIDTHS] + parts + parts + [
            pltpu.VMEM((rows, pw * NAUX), jnp.bfloat16) for pw in WIDTHS] + [
            pltpu.VMEM(amplitudes.shape, jnp.bfloat16),
            pltpu.VMEM((NAUX * nt + 1, span + 16, span), jnp.bfloat16),
            pltpu.VMEM((NAUX, 16, LANES), jnp.float32),
            pltpu.VMEM((rows, aux_part * NAUX), jnp.float32),
            pltpu.VMEM((2, 8, LANES), jnp.int32),
            pltpu.SMEM((2, 8, LANES), jnp.int32),
            pltpu.VMEM((rows, aux_part * NAUX), jnp.bfloat16),
            pltpu.SMEM(partners.shape[::-1], jnp.int32),
            pltpu.SMEM(tile_pos.shape[::-1], jnp.int32),
            dma((6 + CHUNKS,)),
            dma((CHUNKS,)),
            dma((CHUNKS,)),
            dma((CHUNKS, max(PIECES))),
            dma((CHUNKS, max(PIECES))),
            dma((CHUNKS, max(PIECES) // 2)),
            dma((CHUNKS, max(PIECES) // 2)),
            dma((CHUNKS,)),
            dma((5,)),
            dma((NZ,)),
            dma((NZ,)),
            dma((NZ,)),
            dma((NZ,)),
            dma((1,)),
            dma((CHUNKS, SUBS)),
            dma((CHUNKS, SUBS)),
            pltpu.SemaphoreType.REGULAR((WAVES + 2,)),
        ],
        compiler_params=pltpu.CompilerParams(
            collective_id=0, has_side_effects=True, vmem_limit_bytes=60 * 1024 * 1024),
    )(jnp.swapaxes(factors, 1, 2), amplitudes, partners.T, metric_tiles, tile_pos.T)
    return result.reshape(own, rows // own, aux_part * NAUX)


def solution(mesh):
    in_specs = (
        P("orb", None, "aux"),
        P("orb", None, None, None),
        P("orb", None),
        P("aux", None, None),
        P("aux", None),
    )
    out_specs = P("orb", "aux", None)
    return jax.shard_map(shards, mesh=mesh, in_specs=in_specs, out_specs=out_specs, check_vma=False)
```
